32 devices in a mesh: seq: 8 (over z, x), tp: 4 (over y, core).
Axes of the slice: x: 2, y: 2, z: 4, core: 2. Of those that a mesh axis runs over, the one named last changes fastest.
Arguments:
- inputs: bfloat16 [8, 1024, 1024], P('seq', 'tp'), may hold values from -6 to 6
- live_tokens: int32 [8], P('seq'), may hold values from 512 to 1024, as said below
- segments: int32 [8, 1024], P('seq'), may hold values from 0 to 7, never falling along the last dimension, each value on 1 to 512 neighbouring positions
- query_diag: bfloat16 [1024, 1024], P(None, 'tp'), may hold values from -0.1875 to 0.1875
- key_diag: bfloat16 [1024, 1024], P(None, 'tp'), may hold values from -0.1875 to 0.1875
- value_diag: bfloat16 [1024, 1024], P(None, 'tp'), may hold values from -0.1875 to 0.1875
- out_diag: bfloat16 [1024, 1024], P('tp'), may hold values from -0.5 to 0.5
- left_first: bfloat16 [1024, 2816], P(None, 'tp'), may hold values from -0.1875 to 0.1875
- right_first: bfloat16 [1024, 2816], P(None, 'tp'), may hold values from -0.1875 to 0.1875
- down_first: bfloat16 [2816, 1024], P('tp'), may hold values from -0.109375 to 0.109375
- query_norm: bfloat16 [1024, 1024], P(None, 'tp'), may hold values from -0.1875 to 0.1875
- key_norm: bfloat16 [1024, 1024], P(None, 'tp'), may hold values from -0.1875 to 0.1875
- value_norm: bfloat16 [1024, 1024], P(None, 'tp'), may hold values from -0.1875 to 0.1875
- gate_norm: bfloat16 [1024, 1024], P(None, 'tp'), may hold values from -0.1875 to 0.1875
- out_norm: bfloat16 [1024, 1024], P('tp'), may hold values from -0.1875 to 0.1875
- left_second: bfloat16 [1024, 2816], P(None, 'tp'), may hold values from -0.1875 to 0.1875
- right_second: bfloat16 [1024, 2816], P(None, 'tp'), may hold values from -0.1875 to 0.1875
- down_second: bfloat16 [2816, 1024], P('tp'), may hold values from -0.109375 to 0.109375
- cotangent: bfloat16 [8, 1024, 1024], P('seq', 'tp'), may hold values from -6 to 6
Outputs:
- result: bfloat16 [8, 1024, 1024], P('seq', 'tp')
- grad_input: float32 [8, 1024, 1024], P('seq', 'tp')
- grad_query_diag: float32 [1024, 1024], P(None, 'tp')
- grad_key_diag: float32 [1024, 1024], P(None, 'tp')
- grad_value_diag: float32 [1024, 1024], P(None, 'tp')
- grad_out_diag: float32 [1024, 1024], P('tp')
- grad_left_first: float32 [1024, 2816], P(None, 'tp')
- grad_right_first: float32 [1024, 2816], P(None, 'tp')
- grad_down_first: float32 [2816, 1024], P('tp')
- grad_query_norm: float32 [1024, 1024], P(None, 'tp')
- grad_key_norm: float32 [1024, 1024], P(None, 'tp')
- grad_value_norm: float32 [1024, 1024], P(None, 'tp')
- grad_gate_norm: float32 [1024, 1024], P(None, 'tp')
- grad_out_norm: float32 [1024, 1024], P('tp')
- grad_left_second: float32 [1024, 2816], P(None, 'tp')
- grad_right_second: float32 [1024, 2816], P(None, 'tp')
- grad_down_second: float32 [2816, 1024], P('tp')
The draws below stay inside these ranges and needn't reach their ends.
Inputs may be any that keep to these rules, and one draw needn't show every extreme that they name: `live_tokens`: the live positions are a prefix of each bucket, the rest is padding; in every draw some bucket is full. `segments`: segment ids never fall along a bucket; one segment holds at most 512 positions.
All inputs are finite; a program needn't handle non-finite values.
Results may differ from the reference program's by a relative error of at most 0.035.
Values may be sent and summed in bfloat16 or wider, within the bound.
No kernel may reach another device: no remote copies, remote signals or barrier semaphores. Data moves between devices by JAX's collectives and lax.ppermute only.
A program may use at most 192 MiB of HBM per device.

```python
import math
import jax
import jax.numpy as jnp
import numpy as np
from jax import lax

D = 1024
HEADS = 16
HD = 64
FF = 2816
DBLOCK = 64
SEGS = 8
BUCKET = 1024
SEG_MOST = 512
BUCKETS = 8
N_TP = 4


def draw_live_tokens(key, part):
    first_key, second_key = jax.random.split(key)
    drawn = jax.random.randint(first_key, (BUCKETS,), BUCKET // 2, BUCKET + 1)
    full_at = jax.random.randint(second_key, (), 0, BUCKETS)
    return jnp.where(jnp.arange(BUCKETS) == full_at, BUCKET, drawn).astype(jnp.int32)


def shard_levels(key, shape, cuts, smallest, high):
    factor_of = 1.0
    for dim, blocks in cuts:
        heights = jax.random.uniform(jax.random.fold_in(jax.random.fold_in(key, 6), dim), (blocks,), jnp.float32, smallest / len(cuts), high / len(cuts))
        factor_of = factor_of * jnp.repeat(jnp.exp(heights), shape[dim] // blocks).reshape((-1,) + (1,) * (len(shape) - 1 - dim))
    return factor_of


def profile(amount, total, bound, slope):
    loads = [(1 << 20) // math.isqrt(grade ** slope) + 1 for grade in range(2, amount + 1)]
    surplus, counts = total - bound - (amount - 1), [1] * (amount - 1)
    while surplus > 0:
        movable = [i for i in range(amount - 1) if counts[i] < bound]
        mass, remaining = sum([loads[i] for i in movable]), surplus
        for i in movable:
            more = min(bound - counts[i], max(1, remaining * loads[i] // mass), surplus)
            counts[i] = counts[i] + more
            surplus = surplus - more
    return np.array([bound] + counts)


def uneven_parts(own_key, number_of, total, reach, skew):
    if number_of == 2:
        one = jax.random.randint(own_key, (), max(1, total - reach), min(reach, total - 1) + 1)
        return jnp.stack([one, total - one])
    lengths = jnp.asarray(profile(number_of, total, reach, skew), jnp.int32)
    twos = (number_of - 1) // 2
    giver, receiver = lengths[1:1 + 2 * twos:2], lengths[2:2 + 2 * twos:2]
    room = jnp.minimum(giver - 1, reach - receiver)
    moved = jax.random.randint(jax.random.fold_in(own_key, 1), (twos,), 0, 1 << 20) % (room + 1)
    lengths = lengths.at[1:1 + 2 * twos:2].set(giver - moved).at[2:2 + 2 * twos:2].set(receiver + moved)
    return lengths[jax.random.permutation(jax.random.fold_in(own_key, 2), number_of)]


def noise(rng, shape, scale, limit, cuts=(), dtype=jnp.bfloat16):
    entries = scale * jax.random.normal(rng, shape, jnp.float32)
    if cuts:
        entries = entries * shard_levels(rng, shape, cuts, -0.22, 0.18)
    return jnp.clip(entries, -limit, limit).astype(dtype)


def setup_inputs(seed: int = 0) -> dict:
    streams_of = jax.random.split(jax.random.key(seed), 20)
    return {
        "inputs": noise(streams_of[0], (BUCKETS, BUCKET, D), 1.0, 6.0, ((0, 8), (1, 4))),
        "live_tokens": draw_live_tokens(jax.random.fold_in(streams_of[19], 71), 0),
        "segments": jax.vmap(lambda own: jnp.searchsorted(jnp.cumsum(uneven_parts(own, SEGS, BUCKET, SEG_MOST, 2)), jnp.arange(BUCKET), side="right"))(jax.random.split(streams_of[2], BUCKETS)).reshape((BUCKETS, BUCKET)).astype(jnp.int32),
        "query_diag": noise(streams_of[3], (D, D), D ** -0.5, 0.1875, ((1, 4),)),
        "key_diag": noise(streams_of[4], (D, D), D ** -0.5, 0.1875, ((1, 4),)),
        "value_diag": noise(streams_of[5], (D, D), D ** -0.5, 0.1875, ((1, 4),)),
        "out_diag": noise(streams_of[6], (D, D), (D // 8) ** -0.5, 0.5, ((0, 4),)),
        "left_first": noise(streams_of[7], (D, FF), D ** -0.5, 0.1875, ((1, 4),)),
        "right_first": noise(streams_of[8], (D, FF), D ** -0.5, 0.1875, ((1, 4),)),
        "down_first": noise(streams_of[9], (FF, D), FF ** -0.5, 0.109375, ((0, 4),)),
        "query_norm": noise(streams_of[10], (D, D), D ** -0.5, 0.1875, ((1, 4),)),
        "key_norm": noise(streams_of[11], (D, D), D ** -0.5, 0.1875, ((1, 4),)),
        "value_norm": noise(streams_of[12], (D, D), D ** -0.5, 0.1875, ((1, 4),)),
        "gate_norm": noise(streams_of[13], (D, D), D ** -0.5, 0.1875, ((1, 4),)),
        "out_norm": noise(streams_of[14], (D, D), D ** -0.5, 0.1875, ((0, 4),)),
        "left_second": noise(streams_of[15], (D, FF), D ** -0.5, 0.1875, ((1, 4),)),
        "right_second": noise(streams_of[16], (D, FF), D ** -0.5, 0.1875, ((1, 4),)),
        "down_second": noise(streams_of[17], (FF, D), FF ** -0.5, 0.109375, ((0, 4),)),
        "cotangent": noise(streams_of[18], (BUCKETS, BUCKET, D), 1.0, 6.0, ((0, 8), (1, 4))),
    }


epsilon = 1e-06
masked_score = -1e+30
highest = lax.Precision.HIGHEST

@jax.custom_vjp
def low(v):
    return lax.optimization_barrier(v.astype(jnp.bfloat16)).astype(jnp.float32)

@jax.custom_vjp
def low_back(v):
    return v

def low_keep(v):
    return (low(v), None)

def low_pass(kept, grad):
    return (grad,)

def back_keep(v):
    return (v, None)

def back_low(kept, grad):
    return (low(grad),)
low.defvjp(low_keep, low_pass)
low_back.defvjp(back_keep, back_low)

def both_ways(values):
    return low(low_back(values))

def matmul(left_op, right_op):
    return jnp.dot(left_op, right_op, precision=highest)

def rms_rows(values):
    return values * lax.rsqrt(lax.optimization_barrier(jnp.mean(values * values, axis=-1, keepdims=True)) + epsilon)

def silu(before):
    return before * jax.nn.sigmoid(before)

def project(normed, weights):
    pieces = [[] for weight in weights]
    for member_group in range(N_TP):
        copied = low_back(normed)
        for member, weight in enumerate(weights):
            share_width = weight.shape[1] // N_TP
            lower = member_group * share_width
            pieces[member].append(matmul(copied, weight[:, lower:lower + share_width]))
    return [jnp.concatenate(column_parts, axis=1) for column_parts in pieces]

def combine(mixed_rows, weight):
    share_rows = weight.shape[0] // N_TP
    summed = low(matmul(mixed_rows[:, :share_rows], weight[:share_rows]))
    for member_group in range(1, N_TP):
        lower = member_group * share_rows
        summed = summed + low(matmul(mixed_rows[:, lower:lower + share_rows], weight[lower:lower + share_rows]))
    return low_back(summed)

def diag_mixer(stream, segment_ids, query_w, key_w, value_w, out_w):
    normed = low(rms_rows(stream))
    query_rows, key_rows, value_rows = [both_ways(item) for item in project(normed, [query_w, key_w, value_w])]
    length = stream.shape[0]
    blocks = length // DBLOCK
    shaped = (blocks, DBLOCK, HEADS, HD)
    query_rows = query_rows.reshape(shaped)
    key_rows = key_rows.reshape(shaped)
    value_rows = value_rows.reshape(shaped)
    scores = low_back(jnp.einsum('bihd,bjhd->bhij', query_rows, key_rows, precision=highest) * HD ** (-0.5))
    grouped = segment_ids.reshape(blocks, DBLOCK)
    places = jnp.arange(DBLOCK)
    causal = places[:, None] >= places[None, :]
    allowed = (grouped[:, :, None] == grouped[:, None, :]) & causal
    scores = jnp.where(allowed[:, None], scores, masked_score)
    largest = lax.optimization_barrier(jnp.max(scores, axis=-1, keepdims=True))
    raised = jnp.exp(scores - largest)
    attention = raised / lax.optimization_barrier(jnp.sum(raised, axis=-1, keepdims=True))
    mixed_rows = jnp.einsum('bhij,bjhd->bihd', low(attention), value_rows, precision=highest)
    mixed_rows = both_ways(mixed_rows).reshape(length, D)
    return stream + combine(mixed_rows, out_w)

def decay_mix(query_rows, key_rows, value_rows, segment_ids):
    length = query_rows.shape[0]
    position = jnp.arange(length)
    distance = (position[:, None] - position[None, :]).astype(jnp.float32)
    allowed = (distance >= 0) & (segment_ids[:, None] == segment_ids[None, :])
    rates = 2.0 ** (-8.0 * jnp.arange(HEADS).astype(jnp.float32) / HEADS)

    def one_head(packed):
        query_head, key_head, value_head, head_rate = packed
        scores = low_back(matmul(query_head, key_head.T) * HD ** (-0.5))
        decay = jnp.where(allowed, jnp.exp(-head_rate * jnp.maximum(distance, 0.0)), 0.0)
        return matmul(low(scores * decay), value_head)

    def by_head(values):
        return values.reshape(length, HEADS, HD).transpose(1, 0, 2)
    outputs = lax.map(jax.checkpoint(one_head), (by_head(query_rows), by_head(key_rows), by_head(value_rows), rates))
    return outputs.transpose(1, 0, 2).reshape(length, D)

def norm_mixer(stream, segment_ids, query_w, key_w, value_w, gate_w, out_w):
    normed = low(rms_rows(stream))
    before_query, before_key, value_rows, gate_rows = project(normed, [query_w, key_w, value_w, gate_w])
    query_rows = low(silu(low_back(before_query)))
    key_rows = low(silu(low_back(before_key)))
    value_rows = both_ways(value_rows)
    gate_rows = low_back(gate_rows)
    mixed_rows = low_back(decay_mix(query_rows, key_rows, value_rows, segment_ids))
    normed_out = mixed_rows * lax.rsqrt(lax.optimization_barrier(jnp.mean(mixed_rows * mixed_rows, axis=-1, keepdims=True)) + epsilon)
    gated = low(normed_out * gate_rows)
    return stream + combine(gated, out_w)

def glu_mixer(stream, left_w, right_w, down_w):
    normed = low(rms_rows(stream))
    first_rows, second_rows = project(normed, [left_w, right_w])
    product = low(low_back(first_rows) * low_back(second_rows))
    return stream + combine(product, down_w)

def forward(stream, segment_ids, keep_row, weights):
    stream = diag_mixer(stream, segment_ids, weights[0], weights[1], weights[2], weights[3])
    stream = glu_mixer(stream, weights[4], weights[5], weights[6])
    stream = norm_mixer(stream, segment_ids, weights[7], weights[8], weights[9], weights[10], weights[11])
    stream = glu_mixer(stream, weights[12], weights[13], weights[14])
    return stream * keep_row

def add_pair(first_term, second_term):
    return first_term + second_term

def reference(inputs, live_tokens, segments, query_diag, key_diag, value_diag, out_diag, left_first, right_first, down_first, query_norm, key_norm, value_norm, gate_norm, out_norm, left_second, right_second, down_second, cotangent):
    weights = tuple((weight.astype(jnp.float32) for weight in (query_diag, key_diag, value_diag, out_diag, left_first, right_first, down_first, query_norm, key_norm, value_norm, gate_norm, out_norm, left_second, right_second, down_second)))

    def per_bucket(totals, packed):
        bucket_rows, segment_ids, live_count, grad_rows = packed
        keep_row = (jnp.arange(BUCKET) < live_count).astype(jnp.float32)[:, None]

        def closed(stream, weight_set):
            return forward(stream, segment_ids, keep_row, weight_set)
        output, pullback = jax.vjp(closed, bucket_rows.astype(jnp.float32), weights)
        grad_stream, grad_weights = pullback(grad_rows.astype(jnp.float32))
        totals = jax.tree.map(add_pair, totals, grad_weights)
        return (totals, (output.astype(jnp.bfloat16), grad_stream))
    zeros = tuple((jnp.zeros_like(weight) for weight in weights))
    totals, outputs = lax.scan(per_bucket, zeros, (inputs, segments, live_tokens, cotangent))
    result, grad_input = outputs
    means = tuple((total_grad / BUCKETS for total_grad in totals))
    return (result, grad_input, means[0], means[1], means[2], means[3], means[4], means[5], means[6], means[7], means[8], means[9], means[10], means[11], means[12], means[13], means[14])
```

```python
import jax
import jax.numpy as jnp
from jax import lax
from jax.sharding import PartitionSpec as P

D = 1024
HEADS = 16
HD = 64
DBLOCK = 64
N_TP = 4
RING_MOST = 16

epsilon = 1e-06
masked_score = -1e30
bf16 = jnp.bfloat16
f32 = jnp.float32

CORE = [(t, t ^ 1) for t in range(N_TP)]
ALONG_Y = [(t, t ^ 2) for t in range(N_TP)]


def mm(a, b):
    return jnp.dot(a, b, preferred_element_type=f32)


def mm_t(a, b):
    return lax.dot_general(a, b, (((1,), (1,)), ((), ())), preferred_element_type=f32)


def t_mm(a, b):
    return lax.dot_general(a, b, (((0,), (0,)), ((), ())), preferred_element_type=f32)


def spread(own):
    beside = lax.ppermute(own, "tp", CORE)
    across = lax.ppermute(own, "tp", ALONG_Y)
    corner = lax.ppermute(across, "tp", CORE)
    return [own, beside, across, corner]


def gather(own):
    return jnp.concatenate(spread(own), axis=0)


def collect(parts):
    own, beside, across, corner = parts
    to_pass = lax.ppermute(corner, "tp", CORE)
    pair = (across.astype(f32) + to_pass.astype(f32)).astype(across.dtype)
    from_y = lax.ppermute(pair, "tp", ALONG_Y)
    from_core = lax.ppermute(beside, "tp", CORE)
    return own.astype(f32) + from_core.astype(f32) + from_y.astype(f32)


def collect_rows(rows):
    return collect(jnp.split(rows, N_TP, axis=0))


def other_order(values):
    me = lax.axis_index("tp")
    blocks = values.reshape((N_TP, values.shape[0] // N_TP) + values.shape[1:])
    blocks = jnp.where(me % 2 == 1, blocks[jnp.array([1, 0, 3, 2])], blocks)
    blocks = jnp.where(me >= 2, blocks[jnp.array([2, 3, 0, 1])], blocks)
    return blocks.reshape(values.shape)


def rms_rows(values):
    factor = lax.rsqrt(jnp.mean(values * values, axis=-1, keepdims=True) + epsilon)
    return ((values * factor).astype(bf16), factor)


def rms_back(values, factor, gradient):
    inner_mean = jnp.mean(gradient * values, axis=-1, keepdims=True)
    return factor * gradient - values * (factor * factor * factor) * inner_mean


def silu_slope(before):
    logistic = jax.nn.sigmoid(before)
    return logistic * (1.0 + before * (1.0 - logistic))


def diag_allowed(segment_ids, blocks):
    grouped = segment_ids.reshape(blocks, DBLOCK)
    places = jnp.arange(DBLOCK)
    causal = places[:, None] >= places[None, :]
    return (grouped[:, :, None] == grouped[:, None, :]) & causal


def diag_forward(stream, seg_rel, query_w, key_w, value_w, out_w):
    normed, factor = rms_rows(stream)
    rows = gather(normed)
    length = rows.shape[0]
    blocks = length // DBLOCK
    heads_here = query_w.shape[1] // HD
    shape = (blocks, DBLOCK, heads_here, HD)
    q = mm(rows, query_w).astype(bf16).reshape(shape)
    k = mm(rows, key_w).astype(bf16).reshape(shape)
    v = mm(rows, value_w).astype(bf16).reshape(shape)
    allowed = diag_allowed(seg_rel, blocks)[:, None]
    scores = jnp.einsum("bihd,bjhd->bhij", q, k, preferred_element_type=f32) * HD ** (-0.5)
    scores = jnp.where(allowed, scores, masked_score)
    largest = jnp.max(scores, axis=-1, keepdims=True)
    raised = jnp.exp(scores - largest)
    summed = jnp.sum(raised, axis=-1, keepdims=True)
    attention = raised / summed
    mixed = jnp.einsum("bhij,bjhd->bihd", attention.astype(bf16), v, preferred_element_type=f32)
    mixed = mixed.astype(bf16).reshape(length, heads_here * HD)
    kept = (stream, factor, rows, q, k, v, largest + jnp.log(summed), mixed, allowed)
    return (stream + collect_rows(mm(mixed, out_w).astype(bf16)), kept)


def diag_backward(gradient, kept, query_w, key_w, value_w, out_w):
    stream, factor, rows, q, k, v, log_total, mixed, allowed = kept
    length = rows.shape[0]
    e = gather(gradient.astype(bf16))
    do = mm_t(e, out_w).astype(bf16).reshape(q.shape)
    scores = jnp.einsum("bihd,bjhd->bhij", q, k, preferred_element_type=f32) * HD ** (-0.5)
    scores = jnp.where(allowed, scores, masked_score)
    attention = jnp.exp(scores - log_total)
    dp = jnp.einsum("bihd,bjhd->bhij", do, v, preferred_element_type=f32)
    dv = jnp.einsum("bhij,bihd->bjhd", attention.astype(bf16), do, preferred_element_type=f32)
    ds = attention * (dp - jnp.sum(dp * attention, axis=-1, keepdims=True))
    ds = ds.astype(bf16)
    dq = jnp.einsum("bhij,bjhd->bihd", ds, k, preferred_element_type=f32) * HD ** (-0.5)
    dk = jnp.einsum("bhij,bihd->bjhd", ds, q, preferred_element_type=f32) * HD ** (-0.5)
    flat = (length, q.shape[2] * HD)
    dq = dq.astype(bf16).reshape(flat)
    dk = dk.astype(bf16).reshape(flat)
    dv = dv.astype(bf16).reshape(flat)
    da = (mm_t(dq, query_w) + mm_t(dk, key_w) + mm_t(dv, value_w)).astype(bf16)
    gradient = gradient + rms_back(stream, factor, collect_rows(da))
    grads = jnp.concatenate(
        [t_mm(dq, rows), t_mm(dk, rows), t_mm(dv, rows), t_mm(mixed, e)], axis=0
    ).astype(bf16)
    return (gradient, grads)


def glu_forward(stream, left_w, right_w, down_w):
    normed, factor = rms_rows(stream)
    rows = gather(normed)
    f = mm(rows, left_w)
    g = mm(rows, right_w)
    p = (f * g).astype(bf16)
    kept = (stream, factor, rows, f.astype(bf16), g.astype(bf16), p)
    return (stream + collect_rows(mm(p, down_w).astype(bf16)), kept)


def glu_backward(gradient, e, kept, left_w, right_w, down_w):
    stream, factor, rows, f, g, p = kept
    dp = mm_t(e, down_w)
    df = (dp * g.astype(f32)).astype(bf16)
    dg = (dp * f.astype(f32)).astype(bf16)
    da = (mm_t(df, left_w) + mm_t(dg, right_w)).astype(bf16)
    gradient = gradient + rms_back(stream, factor, collect_rows(da))
    grads = jnp.concatenate([t_mm(df, rows), t_mm(dg, rows), t_mm(p, e)], axis=0).astype(bf16)
    return (gradient, grads)


def decay_block(segment_ids, rates, lower, upper):
    row_places = lower + jnp.arange(upper - lower)
    col_places = jnp.arange(upper)
    distance = (row_places[:, None] - col_places[None, :]).astype(f32)
    allowed = (distance >= 0) & (segment_ids[lower:upper][:, None] == segment_ids[:upper][None, :])
    decayed = jnp.exp(-rates[:, None, None] * jnp.maximum(distance, 0.0)[None])
    return jnp.where(allowed[None], decayed, 0.0)


def norm_forward(stream, segment_ids, query_w, key_w, value_w, gate_w, out_w):
    normed, factor = rms_rows(stream)
    rows = gather(normed)
    length = rows.shape[0]
    heads_here = query_w.shape[1] // HD
    uq = mm(rows, query_w)
    uk = mm(rows, key_w)
    shape = (length, heads_here, HD)
    q = other_order((uq * jax.nn.sigmoid(uq)).astype(bf16)).reshape(shape)
    k = other_order((uk * jax.nn.sigmoid(uk)).astype(bf16)).reshape(shape)
    v = other_order(mm(rows, value_w).astype(bf16)).reshape(shape)
    gate = mm(rows, gate_w)
    first_head = lax.axis_index("tp") * heads_here
    rates = 2.0 ** (-8.0 * (first_head + jnp.arange(heads_here)).astype(f32) / HEADS)
    block_rows = min(512, length)
    outputs = []
    for lower in range(0, length, block_rows):
        upper = lower + block_rows
        decay = decay_block(segment_ids, rates, lower, upper)
        scores = jnp.einsum(
            "ihd,jhd->hij", q[lower:upper], k[:upper], preferred_element_type=f32
        ) * HD ** (-0.5)
        weights = (scores * decay).astype(bf16)
        outputs.append(jnp.einsum("hij,jhd->ihd", weights, v[:upper], preferred_element_type=f32))
    mixed = other_order(jnp.concatenate(outputs, axis=0).reshape(length, heads_here * HD))
    power = collect_rows(jnp.sum(mixed * mixed, axis=-1))
    inverse = lax.rsqrt(power / D + epsilon)[:, None]
    gated = (mixed * gate).astype(bf16)
    branch = inverse * collect_rows(mm(gated, out_w).astype(bf16))
    kept = (stream, factor, rows, uq, uk, q, k, v, gate, mixed, inverse, branch, rates)
    return (stream + branch, kept)


def norm_backward(gradient, kept, segment_ids, query_w, key_w, value_w, gate_w, out_w):
    stream, factor, rows, uq, uk, q, k, v, gate, mixed, inverse, branch, rates = kept
    length = rows.shape[0]
    heads_here = q.shape[1]
    low_grad = gradient.astype(bf16)
    inner = jnp.sum(low_grad.astype(f32) * branch, axis=-1)
    sides = jnp.stack([inverse[:, 0], inner], axis=0)
    e = gather(low_grad)
    sides = jnp.concatenate(spread(sides), axis=1)
    r = sides[0][:, None]
    inner = sides[1][:, None]
    dc = mm_t(e, out_w)
    normed_mix = mixed * r
    dgate = (dc * normed_mix).astype(bf16)
    c = (normed_mix * gate).astype(bf16)
    dm = r * (dc * gate) - mixed * (r * r) * (inner / D)
    dm = other_order(dm.astype(bf16)).reshape(q.shape)
    block_rows = min(512, length)
    query_parts = []
    dk = jnp.zeros(q.shape, f32)
    dv = jnp.zeros(q.shape, f32)
    for lower in range(0, length, block_rows):
        upper = lower + block_rows
        decay = decay_block(segment_ids, rates, lower, upper)
        scores = jnp.einsum(
            "ihd,jhd->hij", q[lower:upper], k[:upper], preferred_element_type=f32
        ) * HD ** (-0.5)
        weights = (scores * decay).astype(bf16)
        dm_block = dm[lower:upper]
        dw = jnp.einsum("ihd,jhd->hij", dm_block, v[:upper], preferred_element_type=f32)
        dv = dv.at[:upper].add(
            jnp.einsum("hij,ihd->jhd", weights, dm_block, preferred_element_type=f32)
        )
        ds = (dw * decay).astype(bf16)
        query_parts.append(
            jnp.einsum("hij,jhd->ihd", ds, k[:upper], preferred_element_type=f32) * HD ** (-0.5)
        )
        dk = dk.at[:upper].add(
            jnp.einsum("hij,ihd->jhd", ds, q[lower:upper], preferred_element_type=f32)
            * HD ** (-0.5)
        )
    width = heads_here * HD
    dq = other_order(jnp.concatenate(query_parts, axis=0).reshape(length, width))
    dk = other_order(dk.reshape(length, width))
    dv = other_order(dv.reshape(length, width)).astype(bf16)
    duq = (dq * silu_slope(uq)).astype(bf16)
    duk = (dk * silu_slope(uk)).astype(bf16)
    da = (mm_t(duq, query_w) + mm_t(duk, key_w) + mm_t(dv, value_w) + mm_t(dgate, gate_w)).astype(
        bf16
    )
    gradient = gradient + rms_back(stream, factor, collect_rows(da))
    grads = jnp.concatenate(
        [t_mm(duq, rows), t_mm(duk, rows), t_mm(dv, rows), t_mm(dgate, rows), t_mm(c, e)], axis=0
    ).astype(bf16)
    return (gradient, grads)


def ring_total(grads):
    n = lax.axis_size("seq")
    order = list(range(0, n, 2)) + list(range(n - 1, 0, -2))
    place = jnp.array([order.index(i) for i in range(n)])[lax.axis_index("seq")]
    up = [(order[i], order[(i + 1) % n]) for i in range(n)]
    ways = ((up, 1), ([(b, a) for a, b in up], -1))
    chunk = grads.shape[0] // n
    half = grads.shape[1] // 2
    blocks = grads.reshape(n, chunk, grads.shape[1])

    def own(way, index):
        start = (index % n, 0, way * half)
        return lax.dynamic_slice(blocks, start, (1, chunk, half))[0]

    sums = [own(way, place - sign) for way, (_, sign) in enumerate(ways)]
    for step in range(n - 1):
        for way, (perm, sign) in enumerate(ways):
            got = lax.ppermute(sums[way], "seq", perm)
            mine = own(way, place - sign * (step + 2))
            sums[way] = (got.astype(f32) + mine.astype(f32)).astype(bf16)
    whole = blocks
    for step in range(n):
        for way, (perm, sign) in enumerate(ways):
            if step:
                sums[way] = lax.ppermute(sums[way], "seq", perm)
            start = ((place - sign * step) % n, 0, way * half)
            whole = lax.dynamic_update_slice(whole, sums[way][None], start)
    return whole.reshape(grads.shape)


def seq_total(grads):
    n = lax.axis_size("seq")
    if n <= RING_MOST:
        return ring_total(grads)
    return lax.psum(grads, "seq")


def mean_parts(total, widths, flipped):
    n = lax.axis_size("seq")
    parts = []
    start = 0
    for width, flip in zip(widths, flipped):
        part = total[start : start + width]
        start += width
        parts.append((part.T if flip else part).astype(f32) / n)
    return tuple(parts)


def on_device(
    inputs,
    live_tokens,
    segments,
    query_diag,
    key_diag,
    value_diag,
    out_diag,
    left_first,
    right_first,
    down_first,
    query_norm,
    key_norm,
    value_norm,
    gate_norm,
    out_norm,
    left_second,
    right_second,
    down_second,
    cotangent,
):
    stream = inputs[0].astype(f32)
    segment_ids = segments[0]
    seg_rel = other_order(segment_ids)
    rows_here = stream.shape[0]
    position = lax.axis_index("tp") * rows_here + jnp.arange(rows_here)
    keep_row = (position < live_tokens[0]).astype(f32)[:, None]
    gradient = cotangent[0].astype(f32) * keep_row
    e_second = gather(gradient.astype(bf16))
    stream, kept_diag = diag_forward(stream, seg_rel, query_diag, key_diag, value_diag, out_diag)
    stream, kept_first = glu_forward(stream, left_first, right_first, down_first)
    stream, kept_norm = norm_forward(
        stream, segment_ids, query_norm, key_norm, value_norm, gate_norm, out_norm
    )
    stream, kept_second = glu_forward(stream, left_second, right_second, down_second)
    result = (stream * keep_row).astype(bf16)[None]
    gradient, grads = glu_backward(
        gradient, e_second, kept_second, left_second, right_second, down_second
    )
    ff = left_first.shape[1]
    cols = query_diag.shape[1]
    second = mean_parts(seq_total(grads), (ff, ff, ff), (True, True, False))
    gradient, grads = norm_backward(
        gradient, kept_norm, segment_ids, query_norm, key_norm, value_norm, gate_norm, out_norm
    )
    norm = mean_parts(seq_total(grads), (cols,) * 5, (True,) * 4 + (False,))
    gradient, grads = glu_backward(
        gradient, gather(gradient.astype(bf16)), kept_first, left_first, right_first, down_first
    )
    first = mean_parts(seq_total(grads), (ff, ff, ff), (True, True, False))
    gradient, grads = diag_backward(
        gradient, kept_diag, query_diag, key_diag, value_diag, out_diag
    )
    diag = mean_parts(seq_total(grads), (cols,) * 4, (True,) * 3 + (False,))
    return (result, gradient[None]) + diag + first + norm + second


def solution(mesh):
    rows = P("seq", "tp", None)
    cut_cols = P(None, "tp")
    cut_rows = P("tp", None)
    weights = (
        (cut_cols,) * 3
        + (cut_rows,)
        + (cut_cols,) * 2
        + (cut_rows,)
        + (cut_cols,) * 4
        + (cut_rows,)
        + (cut_cols,) * 2
        + (cut_rows,)
    )
    return jax.shard_map(
        on_device,
        mesh=mesh,
        in_specs=(rows, P("seq"), P("seq", None)) + weights + (rows,),
        out_specs=(rows, rows) + weights,
        check_vma=False,
    )
```

```python
import functools

import jax
import jax.numpy as jnp
from jax import lax
from jax.experimental import pallas as pl
from jax.experimental.pallas import tpu as pltpu
from jax.sharding import PartitionSpec as P


D = 1024
HEADS = 16
HD = 64
DBLOCK = 64
N_TP = 4


epsilon = 1e-06
masked_score = -1e30
bf16 = jnp.bfloat16
f32 = jnp.float32

CORE = [(t, t ^ 1) for t in range(N_TP)]
ALONG_Y = [(t, t ^ 2) for t in range(N_TP)]


def mm(a, b):
    return jnp.dot(a, b, preferred_element_type=f32)


def mm_t(a, b):
    return lax.dot_general(a, b, (((1,), (1,)), ((), ())), preferred_element_type=f32)


def t_mm(a, b):
    return lax.dot_general(a, b, (((0,), (0,)), ((), ())), preferred_element_type=f32)


def spread(own):
    across = lax.ppermute(own, "tp", ALONG_Y)
    beside = lax.ppermute(own, "tp", CORE)
    corner = lax.ppermute(across, "tp", CORE)
    return [own, beside, across, corner]


def collect(parts):
    own, beside, across, corner = parts
    to_pass = lax.ppermute(corner, "tp", CORE)
    pair = (across.astype(f32) + to_pass.astype(f32)).astype(across.dtype)
    from_y = lax.ppermute(pair, "tp", ALONG_Y)
    from_core = lax.ppermute(beside, "tp", CORE)
    return [own, from_core, from_y]


def spread_order(blocks, me):
    b = [blocks[i] for i in range(N_TP)]
    odd = me % 2 == 1
    b = [jnp.where(odd, b[i ^ 1], b[i]) for i in range(N_TP)]
    return jnp.stack([jnp.where(me >= 2, b[i ^ 2], b[i]) for i in range(N_TP)])


TILE = 256
GROUP = 128
VMEM_BYTES = 36 * 1024 * 1024
ANY = pl.BlockSpec(memory_space=pl.ANY)
SMEM = pl.BlockSpec(memory_space=pltpu.SMEM)


def whole(shape):
    return pl.BlockSpec(shape, lambda *i: (0,) * len(shape), pipeline_mode=pl.Buffered(1))


def call(body, grid, ins, in_specs, outs, out_specs, aliases=None, scratch=(), flops=0):
    moved = sum(a.size * a.dtype.itemsize for a in list(ins) + list(outs))
    return pl.pallas_call(
        body,
        grid=grid,
        in_specs=in_specs,
        out_specs=out_specs,
        out_shape=outs,
        input_output_aliases=aliases or {},
        scratch_shapes=list(scratch),
        compiler_params=pltpu.CompilerParams(vmem_limit_bytes=VMEM_BYTES),
        cost_estimate=pl.CostEstimate(flops=flops, bytes_accessed=moved, transcendentals=0),
    )(*ins)


def struct(shape, dtype):
    return jax.ShapeDtypeStruct(shape, dtype)


def head_masks(heads):
    lanes = lax.broadcasted_iota(jnp.int32, (1, heads * HD), 1) // HD
    return [(lanes == h).astype(f32).astype(bf16) for h in range(heads)]


def by_tiles(body, base, tiles, fixed, blocks, made, bufs, flops):
    n_in = len(tiles) + len(fixed) + len(blocks)
    rows = 4 * TILE
    aliases = {}
    ins = list(tiles) + list(fixed) + [b[0] for b in blocks]
    specs = [whole(t.shape) for t in tiles] + [whole(w.shape) for w in fixed]
    specs += [pl.BlockSpec(shape, functools.partial(at, base)) for _, shape, at in blocks]
    outs = [struct((TILE, D), bf16)] * 2 + [struct((rows, w), t) for w, t in made]
    out_specs = [pl.BlockSpec((TILE, D), lambda i: (0, 0))] * 2
    out_specs += [pl.BlockSpec((TILE, w), lambda i: (base + i, 0)) for w, _ in made]
    if bufs is not None:
        ins += list(bufs)
        specs += [ANY] * len(bufs)
        aliases = {n_in + k: 2 + k for k in range(len(bufs))}
    n_bufs = len(bufs) if bufs is not None else 0

    def kernel(*refs):
        i = pl.program_id(0)
        x0, x1 = refs[0], refs[1]
        inner = refs[2:n_in]
        part0, part1 = refs[n_in + n_bufs], refs[n_in + n_bufs + 1]
        keep = refs[n_in + n_bufs + 2 :]

        def run(x_ref, part_ref):
            part_ref[...] = body(x_ref[...], inner, keep).astype(bf16)

        @pl.when(i == 0)
        def _():
            run(x0, part0)

        @pl.when(i == 1)
        def _():
            run(x1, part1)

    got = call(kernel, (2,), ins, specs, outs, out_specs, aliases, flops=flops)
    return list(got[:2]), list(got[2:])


def two_phases(body, blocks4, fixed, blocks, made, flops):
    own, beside, across, corner = blocks4
    near, bufs = by_tiles(body, 0, [own, beside], fixed, blocks, made, None, flops)
    far, bufs = by_tiles(body, 2, [across, corner], fixed, blocks, made, bufs, flops)
    return near + far, bufs


def tile_rows(array):
    return (array, (TILE, array.shape[1]), lambda base, i: (base + i, 0))


def tile_cols(array):
    return (array, (array.shape[0], TILE), lambda base, i: (0, base + i))


def diag_mask(seg_col, seg_row):
    r = lax.broadcasted_iota(jnp.int32, (GROUP, GROUP), 0)
    c = lax.broadcasted_iota(jnp.int32, (GROUP, GROUP), 1)
    return (r // DBLOCK == c // DBLOCK) & (c <= r) & (seg_col == seg_row)


def diag_weights(q, k, allowed):
    s = jnp.where(allowed, mm_t(q, k) * HD ** (-0.5), masked_score)
    raised = jnp.exp(s - jnp.max(s, axis=-1, keepdims=True))
    return raised / jnp.sum(raised, axis=-1, keepdims=True)


def diag_fwd_body(x, inner, keep):
    wq, wk, wv, wo, seg_col, seg_row = inner
    rows, qs, ks, vs, os = keep
    rows[...] = x
    q = mm(x, wq[...]).astype(bf16)
    k = mm(x, wk[...]).astype(bf16)
    v = mm(x, wv[...]).astype(bf16)
    qs[...] = q
    ks[...] = k
    vs[...] = v
    masks = head_masks(wq.shape[1] // HD)
    mixed = []
    for lower in range(0, TILE, GROUP):
        cut = slice(lower, lower + GROUP)
        allowed = diag_mask(seg_col[cut, :], seg_row[0:1, cut])
        total = jnp.zeros((GROUP, q.shape[1]), f32)
        for mask in masks:
            w = diag_weights(q[cut] * mask, k[cut], allowed)
            total += mm(w.astype(bf16), v[cut] * mask)
        mixed.append(total)
    o = jnp.concatenate(mixed, axis=0).astype(bf16)
    os[...] = o
    return mm(o, wo[...])


def diag_bwd_body(e, inner, keep):
    wq, wk, wv, wo, qs, ks, vs, seg_col, seg_row = inner
    es, dqkv = keep
    es[...] = e
    do = mm_t(e, wo[...]).astype(bf16)
    q, k, v = qs[...], ks[...], vs[...]
    masks = head_masks(wq.shape[1] // HD)
    parts = []
    for lower in range(0, TILE, GROUP):
        cut = slice(lower, lower + GROUP)
        allowed = diag_mask(seg_col[cut, :], seg_row[0:1, cut])
        zero = jnp.zeros((GROUP, q.shape[1]), f32)
        dq, dk, dv = zero, zero, zero
        for mask in masks:
            qm, km, dom = q[cut] * mask, k[cut] * mask, do[cut] * mask
            w = diag_weights(qm, k[cut], allowed)
            dw = mm_t(dom, v[cut])
            ds = (w * (dw - jnp.sum(dw * w, axis=-1, keepdims=True))).astype(bf16)
            dv += t_mm(w.astype(bf16), dom)
            dq += mm(ds, km)
            dk += t_mm(ds, qm)
        parts.append((dq * HD ** (-0.5), dk * HD ** (-0.5), dv))
    dq, dk, dv = [jnp.concatenate(p, axis=0).astype(bf16) for p in zip(*parts)]
    dqkv[...] = jnp.concatenate([dq, dk, dv], axis=1)
    return mm_t(dq, wq[...]) + mm_t(dk, wk[...]) + mm_t(dv, wv[...])


def glu_fwd_body(x, inner, keep):
    wl, wr, wd = inner
    rows, fs, gs, ps = keep
    rows[...] = x
    f = mm_t(x, wl[...])
    g = mm_t(x, wr[...])
    p = (f * g).astype(bf16)
    fs[...] = f.astype(bf16)
    gs[...] = g.astype(bf16)
    ps[...] = p
    return mm(p, wd[...])


def glu_bwd_body(e, inner, keep):
    wl, wr, wd, fs, gs = inner
    es, dfs, dgs = keep
    es[...] = e
    dp = mm_t(e, wd[...])
    df = (dp * gs[...].astype(f32)).astype(bf16)
    dg = (dp * fs[...].astype(f32)).astype(bf16)
    dfs[...] = df
    dgs[...] = dg
    return mm(df, wl[...]) + mm(dg, wr[...])


def silu(before):
    return before * (1.0 / (1.0 + jnp.exp(-before)))


def norm_project_body(x, inner, keep):
    wq, wk, wv, wg = inner
    rows, uqs, uks, qs, ks, vs, gates = keep
    rows[...] = x
    uq = mm(x, wq[...])
    uk = mm(x, wk[...])
    uqs[...] = uq
    uks[...] = uk
    qs[...] = silu(uq).astype(bf16)
    ks[...] = silu(uk).astype(bf16)
    vs[...] = mm(x, wv[...]).astype(bf16)
    gates[...] = mm(x, wg[...])


def norm_project(blocks4, weights):
    cols = weights[0].shape[1]
    made = [(D, bf16), (cols, f32), (cols, f32), (cols, bf16), (cols, bf16), (cols, bf16), (cols, f32)]
    bufs = None
    for base in (0, 2):
        tiles = blocks4[base : base + 2]
        ins = list(tiles) + list(weights)
        specs = [whole(a.shape) for a in ins]
        aliases = {}
        if bufs is not None:
            aliases = {len(ins) + k: k for k in range(len(bufs))}
            ins += bufs
            specs += [ANY] * len(bufs)
        n_in = len(ins)

        def kernel(*refs, n_in=n_in):
            i = pl.program_id(0)
            keep = refs[n_in:]

            @pl.when(i == 0)
            def _():
                norm_project_body(refs[0][...], refs[2:6], keep)

            @pl.when(i == 1)
            def _():
                norm_project_body(refs[1][...], refs[2:6], keep)

        bufs = list(
            call(
                kernel,
                (2,),
                ins,
                specs,
                [struct((4 * TILE, w), t) for w, t in made],
                [pl.BlockSpec((TILE, w), lambda i, base=base: (base + i, 0)) for w, _ in made],
                aliases,
                flops=2 * 2 * TILE * D * 4 * cols,
            )
        )
    return bufs


def tile_decay(i, j, seg_col, seg_row):
    r = lax.broadcasted_iota(jnp.int32, (TILE, TILE), 0)
    c = lax.broadcasted_iota(jnp.int32, (TILE, TILE), 1)
    distance = (i - j) * TILE + r - c
    allowed = (distance >= 0) & (seg_col == seg_row)
    return allowed, jnp.maximum(distance, 0).astype(f32)


FAR_TILES = 2


def norm_mix(me, rates, q, k, v, gate, seg_col, seg_row, out_w, order, bufs):
    cols = q.shape[2]
    heads = cols // HD

    def kernel(me_ref, rate_ref, q_ref, k_ref, v_ref, gate_ref, col_ref, row_ref, w_ref, *rest):
        rest = rest[len(bufs or ()) :]
        part_refs, power_refs, m_ref = rest[:2], rest[2:4], rest[4]
        masks = head_masks(heads)
        me_now = me_ref[0]

        def run(step, tile):
            i = jnp.bitwise_xor(me_now, tile)
            qi = q_ref[tile]
            qm = [qi * mask for mask in masks]
            col = col_ref[tile][:, 0:1]

            def over(j, total):
                jr = jnp.bitwise_xor(j, me_now)
                kj = k_ref[jr]
                vj = v_ref[jr]
                allowed, distance = tile_decay(i, j, col, row_ref[jr][0:1, :])
                for h, mask in enumerate(masks):
                    decay = jnp.where(allowed, jnp.exp(-rate_ref[h] * distance), 0.0)
                    w = (mm_t(qm[h], kj) * HD ** (-0.5) * decay).astype(bf16)
                    total += mm(w, vj * mask)
                return total

            low = jnp.maximum(i - FAR_TILES, 0)
            m = lax.fori_loop(low, i + 1, over, jnp.zeros((TILE, cols), f32))
            m_ref[0] = m
            power_refs[step][...] = lax.dot_general(
                jnp.ones((8, cols), f32),
                m * m,
                (((1,), (1,)), ((), ())),
                precision=lax.Precision.HIGHEST,
                preferred_element_type=f32,
            )
            part_refs[step][...] = mm((m * gate_ref[tile]).astype(bf16), w_ref[...]).astype(bf16)

        for step, tile in enumerate(order):
            pl.when(pl.program_id(0) == step)(functools.partial(run, step, tile))

    ins = [me, rates, q, k, v, gate, seg_col, seg_row, out_w]
    specs = [SMEM, SMEM] + [whole(a.shape) for a in ins[2:]]
    aliases = {}
    if bufs is not None:
        ins += bufs
        specs += [ANY]
        aliases = {9: 4}
    first, step = order[0], order[1] - order[0]
    got = call(
        kernel,
        (2,),
        ins,
        specs,
        [struct((TILE, D), bf16)] * 2 + [struct((8, TILE), f32)] * 2 + [struct(gate.shape, f32)],
        [pl.BlockSpec((TILE, D), lambda i: (0, 0))] * 2
        + [pl.BlockSpec((8, TILE), lambda i: (0, 0))] * 2
        + [pl.BlockSpec((1, TILE, cols), lambda i: (first + step * i, 0, 0))],
        aliases,
        flops=2 * TILE * TILE * cols * 2 * heads * 5,
    )
    return got[:2], got[2:4], got[4]


def norm_open_body(e, inner, keep):
    wo, ms, gates, sides = inner
    es, dgates, cs, dms = keep
    es[...] = e
    r = sides[:, 0:1]
    inside = sides[:, 1:2]
    dc = mm_t(e, wo[...])
    m = ms[...]
    gate = gates[...]
    normed = m * r
    dgates[...] = (dc * normed).astype(bf16)
    cs[...] = (normed * gate).astype(bf16)
    dms[...] = (r * (dc * gate) - m * (r * r) * (inside * (1.0 / D))).astype(bf16)


def norm_open(blocks4, out_w, m, gate, sides):
    cols = out_w.shape[0]
    made = [(D, bf16), (cols, bf16), (cols, bf16), (cols, bf16)]
    bufs = None
    for base in (0, 2):
        ins = list(blocks4[base : base + 2]) + [out_w, m, gate, sides]
        specs = [whole(a.shape) for a in ins[:3]]
        specs += [
            pl.BlockSpec((TILE, a.shape[1]), lambda i, base=base: (base + i, 0)) for a in ins[3:]
        ]
        aliases = {}
        if bufs is not None:
            aliases = {6 + k: k for k in range(len(bufs))}
            ins += bufs
            specs += [ANY] * len(bufs)
        n_in = len(ins)

        def kernel(*refs, n_in=n_in):
            i = pl.program_id(0)
            keep = refs[n_in:]

            @pl.when(i == 0)
            def _():
                norm_open_body(refs[0][...], refs[2:6], keep)

            @pl.when(i == 1)
            def _():
                norm_open_body(refs[1][...], refs[2:6], keep)

        bufs = list(
            call(
                kernel,
                (2,),
                ins,
                specs,
                [struct((4 * TILE, w), t) for w, t in made],
                [pl.BlockSpec((TILE, w), lambda i, base=base: (base + i, 0)) for w, _ in made],
                aliases,
                flops=2 * 2 * TILE * D * cols,
            )
        )
    return bufs


def norm_unmix(me, rates, q, k, v, dm, uq, uk, dgate, seg_col, seg_row):
    tiles, _, cols = q.shape
    heads = cols // HD

    def kernel(
        me_ref, rate_ref, q_ref, k_ref, v_ref, dm_ref, uq_ref, uk_ref, dgate_ref, col_ref, row_ref,
        out_ref, dk_sum, dv_sum,
    ):
        masks = head_masks(heads)
        me_now = me_ref[0]
        dk_sum[...] = jnp.zeros_like(dk_sum)
        dv_sum[...] = jnp.zeros_like(dv_sum)

        def slope(before):
            logistic = 1.0 / (1.0 + jnp.exp(-before))
            return logistic * (1.0 + before * (1.0 - logistic))

        def over_rows(i, _):
            ir = jnp.bitwise_xor(i, me_now)
            qi = q_ref[ir]
            dmi = dm_ref[ir]
            col = col_ref[ir][:, 0:1]

            def over(j, dq):
                jr = jnp.bitwise_xor(j, me_now)
                kj = k_ref[jr]
                vj = v_ref[jr]
                allowed, distance = tile_decay(i, j, col, row_ref[jr][0:1, :])
                dk = dk_sum[jr]
                dv = dv_sum[jr]
                for h, mask in enumerate(masks):
                    qm = qi * mask
                    dmm = dmi * mask
                    decay = jnp.where(allowed, jnp.exp(-rate_ref[h] * distance), 0.0)
                    w = (mm_t(qm, kj) * HD ** (-0.5) * decay).astype(bf16)
                    ds = (mm_t(dmm, vj) * decay).astype(bf16)
                    dv += t_mm(w, dmm)
                    dk += t_mm(ds, qm)
                    dq += mm(ds, kj * mask)
                dk_sum[jr] = dk
                dv_sum[jr] = dv
                return dq

            low = jnp.maximum(i - FAR_TILES, 0)
            dq = lax.fori_loop(low, i + 1, over, jnp.zeros((TILE, cols), f32))
            out_ref[ir, :, :cols] = (dq * HD ** (-0.5) * slope(uq_ref[ir])).astype(bf16)
            return 0

        lax.fori_loop(0, tiles, over_rows, 0)
        for tile in range(tiles):
            duk = dk_sum[tile] * HD ** (-0.5) * slope(uk_ref[tile])
            out_ref[tile, :, cols : 2 * cols] = duk.astype(bf16)
            out_ref[tile, :, 2 * cols : 3 * cols] = dv_sum[tile].astype(bf16)
            out_ref[tile, :, 3 * cols :] = dgate_ref[tile]

    ins = [me, rates, q, k, v, dm, uq, uk, dgate, seg_col, seg_row]
    return call(
        kernel,
        (1,),
        ins,
        [SMEM, SMEM] + [whole(a.shape) for a in ins[2:]],
        [struct(q.shape[:2] + (4 * cols,), bf16)],
        [whole(q.shape[:2] + (4 * cols,))],
        scratch=[pltpu.VMEM(q.shape, f32), pltpu.VMEM(q.shape, f32)],
        flops=2 * TILE * TILE * cols * 5 * heads * 9,
    )


def norm_close(grads, weights, base):
    cols = weights[0].shape[1]

    def kernel(*refs):
        i = pl.program_id(0)
        total = None
        for n, w in enumerate(refs[1:5]):
            addend = mm_t(refs[0][:, n * cols : (n + 1) * cols], w[...])
            total = addend if total is None else total + addend

        @pl.when(i == 0)
        def _():
            refs[5][...] = total.astype(bf16)

        @pl.when(i == 1)
        def _():
            refs[6][...] = total.astype(bf16)

    return call(
        kernel,
        (2,),
        [grads] + list(weights),
        [pl.BlockSpec((TILE, 4 * cols), lambda i: (base + i, 0))] + [whole(w.shape) for w in weights],
        [struct((TILE, D), bf16)] * 2,
        [pl.BlockSpec((TILE, D), lambda i: (0, 0))] * 2,
        flops=2 * 2 * TILE * D * cols * 4,
    )


def add_norm(stream, parts, scale=None):
    n = len(parts)

    def kernel(*refs):
        total = refs[1][...].astype(f32)
        for ref in refs[2 : n + 1]:
            total += ref[...].astype(f32)
        rest = refs[n + 1 :]
        if scale is not None:
            total = total * rest[0][...]
            rest = rest[1:]
            rest[2][...] = total
        total = refs[0][...] + total
        rest[0][...] = total
        factor = lax.rsqrt(jnp.mean(total * total, axis=-1, keepdims=True) + epsilon)
        rest[1][...] = (total * factor).astype(bf16)

    ins = [stream] + list(parts) + ([scale] if scale is not None else [])
    outs = [struct(stream.shape, f32), struct(stream.shape, bf16)]
    if scale is not None:
        outs.append(struct(stream.shape, f32))
    half = stream.shape[0] // 2

    def spec(a):
        return pl.BlockSpec((half, a.shape[1]), lambda i: (i, 0))

    return call(kernel, (2,), ins, [spec(a) for a in ins], outs, [spec(a) for a in outs])


def add_norm_back(gradient, stream, parts):
    n = len(parts)

    def kernel(*refs):
        da = refs[2][...].astype(f32)
        for ref in refs[3 : n + 2]:
            da += ref[...].astype(f32)
        v = refs[1][...]
        factor = lax.rsqrt(jnp.mean(v * v, axis=-1, keepdims=True) + epsilon)
        inner_mean = jnp.mean(da * v, axis=-1, keepdims=True)
        total = refs[0][...] + factor * da - v * (factor * factor * factor * inner_mean)
        refs[n + 2][...] = total
        refs[n + 3][...] = total.astype(bf16)

    ins = [gradient, stream] + list(parts)
    outs = [struct(stream.shape, f32), struct(stream.shape, bf16)]
    half = stream.shape[0] // 2

    def spec(a):
        return pl.BlockSpec((half, a.shape[1]), lambda i: (i, 0))

    return call(kernel, (2,), ins, [spec(a) for a in ins], outs, [spec(a) for a in outs])


ON_GRID = 8
COLUMN = (0, 1, 3, 2)
ALONG_X = [(i, i ^ 1) for i in range(ON_GRID)]
ALONG_Z = [(COLUMN[k] * 2 + x, COLUMN[(k + 1) % 4] * 2 + x) for k in range(4) for x in range(2)]


def low_sum(a, b):
    return (a.astype(f32) + b.astype(f32)).astype(bf16)


def assemble(pieces, place):
    shape = pieces[0].shape

    def kernel(place_ref, *refs):
        for n in range(4):

            @pl.when(pl.program_id(0) == n)
            def _(n=n):
                refs[4][...] = refs[n][...]

    return pl.pallas_call(
        kernel,
        name="assemble",
        grid_spec=pltpu.PrefetchScalarGridSpec(
            num_scalar_prefetch=1,
            grid=(4,),
            in_specs=[pl.BlockSpec(shape, lambda i, p: (0, 0), pipeline_mode=pl.Buffered(1))] * 4,
            out_specs=pl.BlockSpec(shape, lambda i, p: (lax.rem(p[0] + 4 - i, 4), 0)),
        ),
        out_shape=struct((4 * shape[0], shape[1]), bf16),
        compiler_params=pltpu.CompilerParams(vmem_limit_bytes=16 * 1024 * 1024),
        cost_estimate=pl.CostEstimate(
            flops=0, bytes_accessed=8 * shape[0] * shape[1] * 2, transcendentals=0
        ),
    )(place.reshape(1), *pieces)


def seq_total(grads):
    half, width = grads.shape[0] // 2, grads.shape[1]
    if lax.axis_size("seq") != ON_GRID:
        total = lax.psum(grads, "seq")
        return total[:half], total[half:]
    index = lax.axis_index("seq")
    x, z = index % 2, index // 2
    place = jnp.where(z >= 2, 5 - z, z)
    halves = grads.reshape(2, half, width)
    send = lax.dynamic_index_in_dim(halves, 1 - x, 0, keepdims=False)
    keep = lax.dynamic_index_in_dim(halves, x, 0, keepdims=False)
    mine = low_sum(keep, lax.ppermute(send, "seq", ALONG_X))
    blocks = mine.reshape(4, half // 4, width)

    def own(n):
        return lax.dynamic_index_in_dim(blocks, lax.rem(place + 8 - n, 4), 0, keepdims=False)

    piece = own(1)
    for n in range(1, 4):
        piece = low_sum(own(n + 1), lax.ppermute(piece, "seq", ALONG_Z))
    pieces = [piece]
    for _ in range(4, 7):
        pieces.append(lax.ppermute(pieces[-1], "seq", ALONG_Z))
    mine = assemble(pieces, place)
    other = lax.ppermute(mine, "seq", ALONG_X)
    return jnp.where(x == 0, mine, other), jnp.where(x == 0, other, mine)


def wgrad(a, b):
    return t_mm(a, b).astype(bf16)


def mean(total):
    return total.astype(f32) / lax.axis_size("seq")


def on_device(
    inputs,
    live_tokens,
    segments,
    query_diag,
    key_diag,
    value_diag,
    out_diag,
    left_first,
    right_first,
    down_first,
    query_norm,
    key_norm,
    value_norm,
    gate_norm,
    out_norm,
    left_second,
    right_second,
    down_second,
    cotangent,
):
    me = lax.axis_index("tp")
    me_ref = me.reshape(1)
    ff = left_first.shape[1]
    cols = query_diag.shape[1]
    length = segments.shape[1]
    first_head = me * (cols // HD)
    rates = 2.0 ** (-8.0 * (first_head + jnp.arange(cols // HD)).astype(f32) / HEADS)
    seg = spread_order(segments[0].reshape(N_TP, TILE), me)
    seg_col = jnp.broadcast_to(seg.reshape(length, 1), (length, GROUP))
    seg_row = jnp.broadcast_to(seg.reshape(1, length), (8, length))
    seg_col4 = seg_col.reshape(N_TP, TILE, GROUP)
    seg_row4 = jnp.broadcast_to(seg[:, None, :], (N_TP, 8, TILE))
    rows_here = inputs.shape[1]
    position = me * rows_here + jnp.arange(rows_here)
    keep_row = (position < live_tokens[0]).astype(f32)[:, None]

    def tiled(a):
        return a.reshape(N_TP, TILE, a.shape[1])

    def flat(a):
        return a.reshape(length, a.shape[2])

    x0 = inputs[0].astype(f32)
    factor = lax.rsqrt(jnp.mean(x0 * x0, axis=-1, keepdims=True) + epsilon)
    a1 = (x0 * factor).astype(bf16)
    g4 = cotangent[0].astype(f32) * keep_row
    a1, g4, g4_low = lax.optimization_barrier((a1, g4, g4.astype(bf16)))
    segs = [tile_rows(seg_col), tile_cols(seg_row)]
    diag_w = [query_diag, key_diag, value_diag]
    parts, (rows1, q1, k1, v1, o1) = two_phases(
        diag_fwd_body,
        spread(a1),
        diag_w + [out_diag],
        segs,
        [(D, bf16)] + [(cols, bf16)] * 4,
        2 * 2 * TILE * D * cols * 4,
    )
    x1, a2 = add_norm(x0, collect(parts))

    glu_made = [(D, bf16)] + [(ff, bf16)] * 3
    glu_flops = 2 * 2 * TILE * D * ff * 3
    first_w = [left_first.T, right_first.T, down_first]
    parts, (rows2, f1, gg1, p1) = two_phases(
        glu_fwd_body, spread(a2), first_w, [], glu_made, glu_flops
    )
    x2, a3 = add_norm(x1, collect(parts))

    norm_w = [query_norm, key_norm, value_norm, gate_norm]
    e4 = spread(g4_low)
    rows3, uq, uk, q3, k3, v3, gate = norm_project(spread(a3), norm_w)
    mix = (me_ref, rates, tiled(q3), tiled(k3), tiled(v3), tiled(gate), seg_col4, seg_row4, out_norm)
    (corner, across), (corner_power, across_power), m3 = norm_mix(*mix, (3, 2), None)
    (beside, own), (beside_power, own_power), m3 = norm_mix(*mix, (1, 0), [m3])
    m3 = flat(m3)
    power = sum(collect([own_power, beside_power, across_power, corner_power]))
    r3 = lax.rsqrt(power[0] / D + epsilon)[:, None]
    x3, a4, branch = add_norm(x2, collect([own, beside, across, corner]), r3)

    second_w = [left_second.T, right_second.T, down_second]
    parts, (rows4, f2, gg2, p2) = two_phases(
        glu_fwd_body, spread(a4), second_w, [], glu_made, glu_flops
    )

    bwd_made = [(D, bf16)] + [(ff, bf16)] * 2
    x4 = x3 + sum(part.astype(f32) for part in collect(parts))
    result = (x4 * keep_row).astype(bf16)[None]
    parts, (es4, df, dg) = two_phases(
        glu_bwd_body, e4, second_w, [tile_rows(f2), tile_rows(gg2)], bwd_made, glu_flops
    )
    second_in = jnp.concatenate([wgrad(df, rows4), wgrad(dg, rows4)], axis=0)
    second_out = wgrad(p2, es4)
    g3, e3 = add_norm_back(g4, x3, collect(parts))

    inner = jnp.sum(e3.astype(f32) * branch, axis=-1)
    sides = jnp.concatenate(spread(jnp.stack([r3[:, 0], inner])), axis=1).T
    es3, dgate, c3, dm = norm_open(spread(e3), out_norm, m3, gate, sides)
    (dqkvg,) = norm_unmix(
        me_ref, rates, tiled(q3), tiled(k3), tiled(v3), tiled(dm), tiled(uq), tiled(uk),
        tiled(dgate), seg_col4, seg_row4,
    )
    dqkvg = flat(dqkvg)
    far = norm_close(dqkvg, norm_w, 2)
    near = norm_close(dqkvg, norm_w, 0)
    norm_grads = jnp.concatenate([wgrad(dqkvg, rows3), wgrad(c3, es3)], axis=0)
    g2, e2 = add_norm_back(g3, x2, collect(list(near) + list(far)))

    parts, (es2, df, dg) = two_phases(
        glu_bwd_body, spread(e2), first_w, [tile_rows(f1), tile_rows(gg1)], bwd_made, glu_flops
    )
    first_in = jnp.concatenate([wgrad(df, rows2), wgrad(dg, rows2)], axis=0)
    first_out = wgrad(p1, es2)
    g1, e1 = add_norm_back(g2, x1, collect(parts))

    parts, (es1, dqkv) = two_phases(
        diag_bwd_body,
        spread(e1),
        diag_w + [out_diag],
        [tile_rows(q1), tile_rows(k1), tile_rows(v1)] + segs,
        [(D, bf16), (3 * cols, bf16)],
        2 * 2 * TILE * D * cols * 4,
    )
    diag_in = wgrad(dqkv, rows1)
    diag_a = diag_in[: 2 * cols]
    diag_b = jnp.concatenate([diag_in[2 * cols :], wgrad(o1, es1)], axis=0)
    g0, _ = add_norm_back(g1, x0, collect(parts))

    left, right = seq_total(second_in)
    low, high = seq_total(second_out)
    second = (mean(left).T, mean(right).T, mean(jnp.concatenate([low, high], axis=0)))
    low, high = seq_total(norm_grads)
    total = jnp.concatenate([low, high], axis=0)
    norm = tuple(mean(total[n * cols : (n + 1) * cols]).T for n in range(4))
    norm += (mean(total[4 * cols :]),)
    left, right = seq_total(first_in)
    low, high = seq_total(first_out)
    first = (mean(left).T, mean(right).T, mean(jnp.concatenate([low, high], axis=0)))
    q_total, k_total = seq_total(diag_a)
    v_total, out_total = seq_total(diag_b)
    diag = (mean(q_total).T, mean(k_total).T, mean(v_total).T, mean(out_total))

    return (result, g0[None]) + diag + first + norm + second


def solution(mesh):
    rows = P("seq", "tp", None)
    cut_cols = P(None, "tp")
    cut_rows = P("tp", None)
    weights = (
        (cut_cols,) * 3
        + (cut_rows,)
        + (cut_cols,) * 2
        + (cut_rows,)
        + (cut_cols,) * 4
        + (cut_rows,)
        + (cut_cols,) * 2
        + (cut_rows,)
    )

    return jax.shard_map(
        on_device,
        mesh=mesh,
        in_specs=(rows, P("seq"), P("seq", None)) + weights + (rows,),
        out_specs=(rows, rows) + weights,
        check_vma=False,
    )
```
